256 devices in a mesh: ctx: 64 (over x, z, core), grp: 4 (over y).
Axes of the slice: x: 4, y: 4, z: 8, core: 2. Of those that a mesh axis runs over, the one named last changes fastest.
Arguments:
- queries: bfloat16 [32768, 1024], P(('grp', 'ctx')), parts along dimension 0, may hold values from -160 to 160
- key_states: bfloat16 [32768, 128], P(('grp', 'ctx')), parts along dimension 0, may hold values from -7 to 7
- value_states: bfloat16 [32768, 128], P(('grp', 'ctx')), parts along dimension 0, may hold values from -6 to 6
- out_grad: bfloat16 [32768, 1024], P(('grp', 'ctx')), parts along dimension 0, may hold values from -6 to 6
- doc_ids: int32 [32768], P('grp'), parts along dimension 0, may hold values from 0 to 15, never falling along the last dimension, each value on 1 to 1024 neighbouring positions
Outputs:
- attn_out: bfloat16 [32768, 1024], P(('grp', 'ctx')), parts along dimension 0
- query_grad: bfloat16 [32768, 1024], P(('grp', 'ctx')), parts along dimension 0
- key_grad: float32 [32768, 128], P(('grp', 'ctx')), parts along dimension 0
- value_grad: float32 [32768, 128], P(('grp', 'ctx')), parts along dimension 0
The draws below stay inside these ranges and needn't reach their ends.
There are 4 independent parts, one for each index of `grp`. The reference program is written for one: setup_inputs(seed, part) draws one part's arguments, and reference() takes and returns one part's arrays. A program takes and returns all parts, laid end to end along the dimension named above; each array names one. Nothing has to cross between parts.
Inputs may be any that keep to these rules, and one draw needn't show every extreme that they name: `doc_ids`: nondecreasing along the sequence; each document covers 1 to 1024 consecutive tokens, one exactly 1024.
All inputs are finite; a program needn't handle non-finite values.
Results may differ from the reference program's by a relative error of at most 0.03.
Values may be sent and summed in bfloat16 or wider, within the bound.
No kernel may reach another device: no remote copies, remote signals or barrier semaphores. Data moves between devices by JAX's collectives and lax.ppermute only.
A program may use at most 64 MiB of HBM per device.

```python
import math
import jax
import jax.numpy as jnp
import numpy as np
from jax import lax

H = 8
HD = 128
DOCS = 16
STRETCH = 64
SPAN = 16
TOKENS = 8192
MOST = 1024
N_CTX = 64


def shared_keys(key):
    base = jnp.clip(jax.random.normal(jax.random.fold_in(key, 11), (TOKENS, HD), jnp.float32), -6.0, 6.0)
    return base


def draw_key_states(key, part):
    return shared_keys(key).astype(jnp.bfloat16)


def draw_queries(key, part):
    base = jnp.clip(jax.random.normal(jax.random.fold_in(key, 23), (TOKENS, H, HD), jnp.float32), -6.0, 6.0)
    return base.reshape(TOKENS, H * HD).astype(jnp.bfloat16)


def block_levels(own_key, dims, split, low, top_value):
    level, own = 1.0, jax.random.fold_in(own_key, 6)
    for axis_at, parts in split:
        steps = jnp.exp(jax.random.uniform(jax.random.fold_in(own, axis_at), (parts,), jnp.float32, low / len(split), top_value / len(split)))
        level = level * jnp.repeat(steps, dims[axis_at] // parts).reshape([-1 if axis == axis_at else 1 for axis in range(len(dims))])
    return level


def split_up(number_of, total, reach, lean):
    portions = [(1 << 20) // math.isqrt(rank ** lean) + 1 for rank in range(2, number_of + 1)]
    surplus, counts = total - reach - (number_of - 1), [1] * (number_of - 1)
    while surplus > 0:
        free = [i for i in range(number_of - 1) if counts[i] < reach]
        pool, remaining = sum([portions[i] for i in free]), surplus
        for i in free:
            extra = min(reach - counts[i], max(1, remaining * portions[i] // pool), surplus)
            counts[i] = counts[i] + extra
            surplus = surplus - extra
    return np.array([reach] + counts)


def ragged_sizes(stream_key, number_of, total, reach, lean):
    if number_of == 2:
        one = jax.random.randint(stream_key, (), max(1, total - reach), min(reach, total - 1) + 1)
        return jnp.stack([one, total - one])
    tallies = jnp.asarray(split_up(number_of, total, reach, lean), jnp.int32)
    couples = (number_of - 1) // 2
    source_of, receiver = tallies[1:1 + 2 * couples:2], tallies[2:2 + 2 * couples:2]
    slack = jnp.minimum(source_of - 1, reach - receiver)
    passed = jax.random.randint(jax.random.fold_in(stream_key, 1), (couples,), 0, 1 << 20) % (slack + 1)
    tallies = tallies.at[1:1 + 2 * couples:2].set(source_of - passed).at[2:2 + 2 * couples:2].set(receiver + passed)
    return tallies[jax.random.permutation(jax.random.fold_in(stream_key, 2), number_of)]


def scatter_about(stream_key, shape, spread, limit, pieces=(), kind=jnp.bfloat16):
    result = jax.random.normal(stream_key, shape, jnp.float32) * spread
    if len(pieces) > 0:
        result = block_levels(stream_key, shape, pieces, -0.22, 0.18) * result
    return jnp.clip(result, min=-limit, max=limit).astype(kind)


def setup_inputs(seed: int = 0, part: int = 0) -> dict:
    key_list = jax.random.split(jax.random.key(seed), 6)
    part_keys = jax.random.split(jax.random.fold_in(key_list[5], part), 6)
    queries = draw_queries(jax.random.fold_in(jax.random.fold_in(key_list[5], part), 71), part)
    key_states = draw_key_states(jax.random.fold_in(jax.random.fold_in(key_list[5], part), 71), part)
    value_states = scatter_about(part_keys[2], (TOKENS, HD), 1.0, 6.0, ((0, 64),))
    out_grad = scatter_about(part_keys[3], (TOKENS, H * HD), 1.0, 6.0, ((0, 64),))
    doc_ids = jnp.searchsorted(jnp.cumsum(ragged_sizes(part_keys[4], DOCS, TOKENS, MOST, 2)), jnp.arange(TOKENS), side="right").astype(jnp.int32)
    return dict(queries=queries, key_states=key_states, value_states=value_states, out_grad=out_grad, doc_ids=doc_ids)


def window_terms(query_rows, grad_rows, key_win, value_win, query_doc, window_doc):
    row_count = query_rows.shape[0]
    window = key_win.shape[0]
    head_dim = key_win.shape[1]
    head_count = query_rows.shape[1] // head_dim
    offset = window - row_count
    scaling = 1.0 / math.sqrt(head_dim)
    column = lax.broadcasted_iota(jnp.int32, (row_count, window), 1)
    row_index = lax.broadcasted_iota(jnp.int32, (row_count, window), 0)
    allowed = (window_doc[None, :] == query_doc[:, None]) & (column <= row_index + offset)
    allowed = jnp.concatenate([allowed, allowed], axis=0)

    def regroup(array):
        return array.reshape(row_count, head_count, head_dim).transpose(1, 0, 2).reshape(head_count // 2, 2 * row_count, head_dim)

    def one_group(totals, pair_rows):
        key_acc, value_acc = totals
        query_blk, grad_blk = pair_rows
        scores = scaling * jnp.dot(query_blk, key_win.T, preferred_element_type=jnp.float32)
        scores = jnp.where(allowed, scores, -1e+30)
        row_max = lax.optimization_barrier(jnp.max(scores, axis=1, keepdims=True))
        row_sum = lax.optimization_barrier(jnp.sum(jnp.exp(scores - row_max), axis=1, keepdims=True))
        weights = jnp.exp(scores - (row_max + jnp.log(row_sum)))
        prob_bf = weights.astype(jnp.bfloat16)
        out_rows = jnp.dot(prob_bf, value_win, preferred_element_type=jnp.float32).astype(jnp.bfloat16)
        row_dot = lax.optimization_barrier(jnp.sum(grad_blk.astype(jnp.float32) * out_rows.astype(jnp.float32), axis=1, keepdims=True))
        dprobs = jnp.dot(grad_blk, value_win.T, preferred_element_type=jnp.float32)
        dscores = (weights * (dprobs - row_dot)).astype(jnp.bfloat16)
        query_part = (scaling * jnp.dot(dscores, key_win, preferred_element_type=jnp.float32)).astype(jnp.bfloat16)
        key_acc = key_acc + scaling * jnp.dot(dscores.T, query_blk, preferred_element_type=jnp.float32)
        value_acc = value_acc + jnp.dot(prob_bf.T, grad_blk, preferred_element_type=jnp.float32)
        return ((key_acc, value_acc), (out_rows, query_part))
    zeroed = jnp.zeros((window, head_dim), jnp.float32)
    (key_acc, value_acc), (out_all, query_all) = lax.scan(one_group, (zeroed, zeroed), (regroup(query_rows), regroup(grad_rows)))

    def restore(array):
        return array.reshape(head_count, row_count, head_dim).transpose(1, 0, 2).reshape(row_count, head_count * head_dim)
    return (restore(out_all), restore(query_all), key_acc, value_acc)

def pair_order(array):
    blocks = array.reshape(2 * N_CTX, STRETCH, array.shape[1])
    lower_blocks = blocks[:N_CTX]
    upper_blocks = blocks[N_CTX:][::-1]
    return jnp.stack([lower_blocks, upper_blocks], axis=1).reshape(array.shape)

def reference(queries, key_states, value_states, out_grad, doc_ids):
    row_count = STRETCH
    padding = SPAN * STRETCH
    window_len = padding + row_count
    doc_all = doc_ids.astype(jnp.int32)
    key_padded = jnp.concatenate([jnp.zeros((padding, HD), key_states.dtype), key_states], axis=0)
    value_padded = jnp.concatenate([jnp.zeros((padding, HD), value_states.dtype), value_states], axis=0)
    doc_padded = jnp.concatenate([jnp.full((padding,), -1, jnp.int32), doc_all], axis=0)

    def one_block(totals, block_number):
        key_full, value_full = totals
        anchor = (block_number * row_count).astype(jnp.int32)
        query_rows = lax.dynamic_slice_in_dim(queries, anchor, row_count, 0)
        grad_rows = lax.dynamic_slice_in_dim(out_grad, anchor, row_count, 0)
        key_win = lax.dynamic_slice_in_dim(key_padded, anchor, window_len, 0)
        value_win = lax.dynamic_slice_in_dim(value_padded, anchor, window_len, 0)
        window_doc = lax.dynamic_slice_in_dim(doc_padded, anchor, window_len, 0)
        query_doc = lax.dynamic_slice_in_dim(doc_all, anchor, row_count, 0)
        out_rows, query_part, key_acc, value_acc = window_terms(query_rows, grad_rows, key_win, value_win, query_doc, window_doc)
        key_full = lax.dynamic_update_slice_in_dim(key_full, lax.dynamic_slice_in_dim(key_full, anchor, window_len, 0) + key_acc, anchor, 0)
        value_full = lax.dynamic_update_slice_in_dim(value_full, lax.dynamic_slice_in_dim(value_full, anchor, window_len, 0) + value_acc, anchor, 0)
        return ((key_full, value_full), (out_rows, query_part))
    zeroed = jnp.zeros((padding + TOKENS, HD), jnp.float32)
    (key_full, value_full), (out_all, query_all) = lax.scan(one_block, (zeroed, zeroed), jnp.arange(2 * N_CTX, dtype=jnp.int32))
    attn_seq = out_all.reshape(TOKENS, H * HD)
    query_seq = query_all.reshape(TOKENS, H * HD)
    return (pair_order(attn_seq), pair_order(query_seq), pair_order(key_full[padding:]), pair_order(value_full[padding:]))
```

```python
import functools
import math

import jax
import jax.numpy as jnp
from jax import lax
from jax.experimental import pallas as pl
from jax.experimental.pallas import tpu as pltpu
from jax.sharding import PartitionSpec as P


MASKED = -1e30
TILE = 128
BACK = 4
TILES = 2 * BACK + 1
GROUPS = 2


def nt(a, b):
    return lax.dot_general(a, b, (((1,), (1,)), ((), ())), preferred_element_type=jnp.float32)


def nn(a, b):
    return jnp.dot(a, b, preferred_element_type=jnp.float32)


def attention_kernel(last, heads, core_ref, low_ref, q_ref, g_ref, mine_ref, theirs_ref, *rest):
    if last:
        acc_ref, even_ref, odd_ref, keep_ref, give_ref = rest[:5]
    else:
        even_ref, odd_ref, acc_out = rest[:3]
    kt_ref, vt_ref, t_ref, d_ref, p_ref, s_ref = rest[-6:]
    core = core_ref[0]
    dim = TILE
    scaling = 1.0 / math.sqrt(dim)
    to_log2 = scaling * math.log2(math.e)
    half = TILE // 2

    def keys(j):
        return mine_ref[j // 2, :, :dim] if j % 2 == 0 else theirs_ref[j // 2 + core, :, :dim]

    def values(j):
        return mine_ref[j // 2, :, dim:] if j % 2 == 0 else theirs_ref[j // 2 + core, :, dim:]

    for j in range(TILES):
        kt_ref[:, j * TILE : (j + 1) * TILE] = keys(j).T
        vt_ref[:, j * TILE : (j + 1) * TILE] = values(j).T

    low = jnp.concatenate([low_ref[...], low_ref[...]], axis=1)
    row = lax.broadcasted_iota(jnp.int32, (TILE, 2 * TILE), 0)
    lane = lax.broadcasted_iota(jnp.int32, (TILE, 2 * TILE), 1) % TILE

    def stacked(ref, pair):
        cut = 2 * pair * dim
        return jnp.concatenate([ref[:, cut : cut + dim], ref[:, cut + dim : cut + 2 * dim]], axis=0)

    for pair in range(heads // 2):
        q2 = stacked(q_ref, pair)
        g2 = stacked(g_ref, pair)
        top = jnp.full((1, 2 * TILE), MASKED, jnp.float32)
        for j in range(TILES):
            ok = row + j * TILE >= low
            if j == TILES - 1:
                ok = ok & (row <= lane)
            t = jnp.where(ok, nt(keys(j), q2) * to_log2, MASKED)
            t_ref[j * TILE : (j + 1) * TILE, :] = t
            top = jnp.maximum(top, jnp.max(t, axis=0, keepdims=True))
        total = jnp.zeros((1, 2 * TILE), jnp.float32)
        dotted = jnp.zeros((1, 2 * TILE), jnp.float32)
        for j in range(TILES):
            at = slice(j * TILE, (j + 1) * TILE)
            e = jnp.exp2(t_ref[at, :] - top)
            d = nt(values(j), g2)
            t_ref[at, :] = e
            d_ref[at, :] = d
            total = total + jnp.sum(e, axis=0, keepdims=True)
            dotted = dotted + jnp.sum(e * d, axis=0, keepdims=True)
        inverse = 1.0 / total
        row_dot = dotted * inverse
        cols = slice(2 * pair * dim, 2 * (pair + 1) * dim)
        for j in range(TILES):
            at = slice(j * TILE, (j + 1) * TILE)
            w = t_ref[at, :] * inverse
            p_ref[at, cols] = w.astype(jnp.bfloat16)
            s_ref[at, cols] = (w * (d_ref[at, :] - row_dot)).astype(jnp.bfloat16)
        out = nn(vt_ref[...], p_ref[:, cols]).T.astype(jnp.bfloat16)
        dq = (nn(kt_ref[...], s_ref[:, cols]) * scaling).T.astype(jnp.bfloat16)
        for h in range(2):
            for base, block in ((0, out), (heads * dim, dq)):
                at = slice(base + (2 * pair + h) * dim, base + (2 * pair + h + 1) * dim)
                even_ref[:, at] = block[h * TILE : h * TILE + half]
                odd_ref[:, at] = block[h * TILE + half : (h + 1) * TILE]

    q_all = jnp.concatenate([q_ref[:, h * dim : (h + 1) * dim] for h in range(heads)], axis=0)
    g_all = jnp.concatenate([g_ref[:, h * dim : (h + 1) * dim] for h in range(heads)], axis=0)
    if last:
        blank = jnp.zeros((TILE, 2 * dim), give_ref.dtype)
        give_ref[(1 - core) * BACK] = blank
    for j in range(TILES):
        at = slice(j * TILE, (j + 1) * TILE)
        dk = nn(s_ref[at, :], q_all) * scaling
        dv = nn(p_ref[at, :], g_all)
        if not last:
            acc_out[j, :, :dim] = dk
            acc_out[j, :, dim:] = dv
            continue
        dk = dk + acc_ref[j, :, :dim]
        dv = dv + acc_ref[j, :, dim:]
        if j % 2 == 0:
            keep_ref[j // 2, :, :dim] = dk
            keep_ref[j // 2, :, dim:] = dv
        else:
            give_ref[j // 2 + core, :, :dim] = dk.astype(give_ref.dtype)
            give_ref[j // 2 + core, :, dim:] = dv.astype(give_ref.dtype)


def attention(group, core, low, queries, grads, mine, theirs, acc):
    rows = queries.shape[0]
    heads = queries.shape[1] // TILE // GROUPS
    wide = heads * TILE
    last = acc is not None
    full = pl.BlockSpec(memory_space=pltpu.VMEM)
    columns = pl.BlockSpec((rows, wide), lambda i: (0, group))

    def whole(shape):
        return pl.BlockSpec(shape, lambda i: (0,) * len(shape))

    tiles = (BACK + 1, TILE, 2 * TILE)
    acc_shape = (TILES, TILE, 2 * TILE)
    side = (rows // 2, 2 * wide)
    outs = [
        jax.ShapeDtypeStruct(side, jnp.bfloat16),
        jax.ShapeDtypeStruct(side, jnp.bfloat16),
    ]
    if last:
        outs += [
            jax.ShapeDtypeStruct(tiles, jnp.float32),
            jax.ShapeDtypeStruct(tiles, jnp.bfloat16),
        ]
    else:
        outs += [jax.ShapeDtypeStruct(acc_shape, jnp.float32)]
    ins = [core, low, queries, grads, mine, theirs] + ([acc] if last else [])
    specs = [
        pl.BlockSpec(memory_space=pltpu.SMEM),
        whole((1, rows)),
        columns,
        columns,
        whole(tiles),
        whole(tiles),
    ] + ([whole(acc_shape)] if last else [])
    span = TILES * TILE
    work = 2 * wide * span * TILE * 6
    return pl.pallas_call(
        functools.partial(attention_kernel, last, heads),
        grid=(1,),
        in_specs=specs,
        out_specs=[whole(o.shape) for o in outs],
        out_shape=outs,
        scratch_shapes=[
            pltpu.VMEM((TILE, span), jnp.bfloat16),
            pltpu.VMEM((TILE, span), jnp.bfloat16),
            pltpu.VMEM((span, 2 * TILE), jnp.float32),
            pltpu.VMEM((span, 2 * TILE), jnp.float32),
            pltpu.VMEM((span, wide), jnp.bfloat16),
            pltpu.VMEM((span, wide), jnp.bfloat16),
        ],
        cost_estimate=pl.CostEstimate(
            flops=work, bytes_accessed=4 * 1024 * 1024, transcendentals=wide * span
        ),
    )(*ins)


def shards(queries, key_states, value_states, out_grad, doc_ids):
    members = lax.axis_size("ctx")
    device = lax.axis_index("ctx")
    rows = queries.shape[0]
    half = rows // 2
    dim = key_states.shape[1]
    core = device % 2
    even = core == 0

    def chips(distance):
        return [(i, (i + 2 * distance) % members) for i in range(members)]

    partner = [(i, i ^ 1) for i in range(members)]
    middle = members // 2
    even_block = [(i, 2 * i if i < middle else 2 * members - 1 - 2 * i) for i in range(members)]
    odd_block = [(i, 2 * i + 1 if i < middle else 2 * members - 2 - 2 * i) for i in range(members)]

    def move(array, route):
        return lax.ppermute(array, "ctx", route)

    def settle(first, second):
        return jnp.where(even, first, second), jnp.where(even, second, first)

    pair = jnp.concatenate([key_states, value_states], axis=1)
    mine = jnp.stack([move(pair, chips(n)) for n in range(BACK, 0, -1)] + [pair])
    theirs = move(mine, partner)

    reach = (TILES - 1) * TILE
    padded = jnp.concatenate([jnp.full((reach,), -1, jnp.int32), doc_ids])
    window = lax.dynamic_slice_in_dim(padded, device * rows, reach + rows, 0)
    low = jnp.sum((window[:, None] < window[None, reach:]).astype(jnp.int32), axis=0)[None, :]
    parity = core.astype(jnp.int32)[None]

    sides = []
    acc = None
    for group in range(GROUPS):
        result = attention(group, parity, low, queries, out_grad, mine, theirs, acc)
        sides.append((move(result[0], even_block), move(result[1], odd_block)))
        acc = result[2]
    keep, give = result[2:]
    total = keep + move(give, partner).astype(jnp.float32)
    own = total[BACK]
    for n in range(1, BACK + 1):
        own = own + move(total[BACK - n].astype(jnp.bfloat16), chips(-n)).astype(jnp.float32)
    own = own.astype(jnp.bfloat16)
    grads = settle(move(own[:half], even_block), move(own[half:], odd_block))
    grads = jnp.concatenate(grads, axis=0).astype(jnp.float32)

    settled = [settle(*side) for side in sides]
    wide = queries.shape[1] // GROUPS
    outs = []
    for base in (0, wide):
        slots = [
            jnp.concatenate([block[slot][:, base : base + wide] for block in settled], axis=1)
            for slot in range(2)
        ]
        outs.append(jnp.concatenate(slots, axis=0))
    return outs[0], outs[1], grads[:, :dim], grads[:, dim:]


def solution(mesh):
    split = P(("grp", "ctx"), None)
    return jax.shard_map(
        shards,
        mesh=mesh,
        in_specs=(split, split, split, split, P("grp")),
        out_specs=(split, split, split, split),
        check_vma=False,
    )
```
